512 devices in a mesh: row: 32 (over y_hi, z), col: 16 (over y_lo, x, core).
Axes of the slice: x: 4, y: 4 (y_hi: 2, y_lo: 2; y = y_hi * 2 + y_lo), z: 16, core: 2. Of those that a mesh axis runs over, the one named last changes fastest.
Arguments:
- diag_block: float32 [512, 512], replicated, as said below
- panel: float32 [32768, 512], P('row', 'col'), may hold values from -2 to 2
- tiles: float32 [14336, 128, 128], P(('row', 'col')), may hold values from -6 to 6
- targets: int32 [14336, 2], P(('row', 'col')), may hold values from 0 to 255, as said below
Outputs:
- panel_factor: float32 [32768, 512], P('row', 'col')
- schur_tiles: float32 [14336, 128, 128], P(('row', 'col'))
The draws below stay inside these ranges and needn't reach their ends.
Inputs may be any that keep to these rules, and one draw needn't show every extreme that they name: `diag_block`: symmetric positive definite. `targets`: slot s belongs to the device d = s // 28 at grid row d // 16 and grid column d % 16; its p satisfies p // 8 == d // 16 and its q satisfies (q // 8) % 16 == d % 16.
All inputs are finite; a program needn't handle non-finite values.
Results may differ from the reference program's by a relative error of at most 0.0003.
Values sent between devices are 32-bit elements; how exact they have to be, the bound alone decides.
No kernel may reach another device: no remote copies, remote signals or barrier semaphores. Data moves between devices by JAX's collectives and lax.ppermute only.
A program may use at most 128 MiB of HBM per device.

```python
import jax
import jax.numpy as jnp
from jax import lax

W = 512
TB = 128
NBD = 8
TPD = 28
NB = 256
TILES = 14336
N_ROW = 32
N_COL = 16


def draw_diag_block(key, part):
    factor = jax.random.normal(jax.random.fold_in(key, 11), (W, W), jnp.float32)
    matrix = jnp.dot(factor, factor.T, precision=lax.Precision.HIGHEST) / W + 0.5 * jnp.eye(W, dtype=jnp.float32)
    return matrix


def draw_targets(key, part):
    slots = jnp.arange(TILES, dtype=jnp.int32)
    device = slots // TPD
    grid_row = device // N_COL
    grid_col = device % N_COL
    first_local = jax.random.randint(jax.random.fold_in(key, 21), (TILES,), 0, NBD, dtype=jnp.int32)
    second_group = jax.random.randint(jax.random.fold_in(key, 22), (TILES,), 0, N_ROW // N_COL, dtype=jnp.int32)
    second_local = jax.random.randint(jax.random.fold_in(key, 23), (TILES,), 0, NBD, dtype=jnp.int32)
    row_block = grid_row * NBD + first_local
    col_block = (grid_col + N_COL * second_group) * NBD + second_local
    return jnp.stack([row_block, col_block], axis=1).astype(jnp.int32)


def steps_of(rng, extent, split, low, largest):
    def one(position, blocks):
        draws = jax.random.uniform(jax.random.fold_in(jax.random.fold_in(rng, 6), position), (blocks,), jnp.float32, low / len(split), largest / len(split))
        return jnp.repeat(jnp.exp(draws), extent[position] // blocks).reshape((-1,) + (1,) * (len(extent) - position - 1))

    gain = one(*split[0])
    for cut in split[1:]:
        gain = gain * one(*cut)
    return gain


def gaussian(stream_key, shape, deviation, bound, cuts=(), kind=jnp.bfloat16):
    drawn = jax.random.normal(stream_key, shape, jnp.float32) * deviation
    if len(cuts) > 0:
        drawn = steps_of(stream_key, shape, cuts, -0.22, 0.18) * drawn
    return jnp.clip(drawn, min=-bound, max=bound).astype(kind)


def setup_inputs(seed: int = 0) -> dict:
    arg_keys = jax.random.split(jax.random.key(seed), 5)
    return {
        "diag_block": draw_diag_block(jax.random.fold_in(arg_keys[4], 71), 0),
        "panel": gaussian(arg_keys[1], (NB * TB, W), 0.25, 2.0, ((0, 32), (1, 16)), jnp.float32),
        "tiles": gaussian(arg_keys[2], (TILES, TB, TB), 1.0, 6.0, ((0, 512),), jnp.float32),
        "targets": draw_targets(jax.random.fold_in(arg_keys[4], 71), 0),
    }


def reference(diag_block, panel, tiles, targets):
    diag_factor = jnp.linalg.cholesky(diag_block)
    panel_factor = jax.scipy.linalg.solve_triangular(diag_factor, panel.T, lower=True).T
    blocks = panel_factor.reshape(NB, TB, W)
    groups = TILES // TPD
    tile_groups = tiles.reshape(groups, TPD, TB, TB)
    target_groups = targets.reshape(groups, TPD, 2)

    def update_group(inputs):
        group_tiles, group_targets = inputs
        left = blocks[group_targets[:, 0]]
        right = blocks[group_targets[:, 1]]
        update = jnp.einsum('skw,slw->skl', left, right, precision=lax.Precision.HIGHEST)
        keep = group_targets[:, 0] >= group_targets[:, 1]
        return group_tiles - jnp.where(keep[:, None, None], update, jnp.zeros_like(update))
    schur_tiles = lax.map(update_group, (tile_groups, target_groups)).reshape(TILES, TB, TB)
    return (panel_factor, schur_tiles)
```

```python
import jax
import jax.numpy as jnp
from jax import lax
from jax.experimental import pallas as pl
from jax.experimental.pallas import tpu as pltpu
from jax.sharding import PartitionSpec as P

W, B, G = 512, 128, 8
HI = lax.Precision.HIGHEST

def splat(col, k):
    return jnp.broadcast_to(col[k:k + 1, :], (G, B))

def factor_block(groups):
    n = len(groups)
    lane = lax.broadcasted_iota(jnp.int32, (G, B), 1)
    sub = lax.broadcasted_iota(jnp.int32, (G, B), 0)
    out = []
    for g in range(n):
        base = g * G
        rows = groups[g]
        cols = [jnp.broadcast_to(rows[:, base + m:base + m + 1], (G, B)) for m in range(G)]
        a = {(k, m): splat(cols[m], k) for m in range(G) for k in range(m, G)}
        inv = {}
        low = {}
        for m in range(G):
            r = lax.rsqrt(a[m, m])
            inv[m, m] = r
            for k in range(m + 1, G):
                low[k, m] = a[k, m] * r
            for j in range(m + 1, G):
                for k in range(j, G):
                    a[k, j] = a[k, j] - low[k, m] * low[j, m]
            for j in range(m):
                total = low[m, j] * inv[j, j]
                for k in range(j + 1, m):
                    total = total + low[m, k] * inv[k, j]
                inv[m, j] = -total * r
        inside = (lane >= base) & (lane < base + G)
        unit = jnp.where(lane - base == sub, 1.0, 0.0).astype(jnp.float32)
        rows = jnp.where(inside, unit, rows)
        spread = [splat(rows, m) for m in range(G)]
        done = None
        for m in range(G):
            column = inv[m, m]
            for k in range(m + 1, G):
                column = jnp.where(sub == k, inv[k, m], column)
            column = jnp.where(sub < m, 0.0, column)
            term = column * spread[m]
            done = term if done is None else done + term
        out.append(jnp.where(lane < base + G, done, 0.0))
        if g + 1 == n:
            break
        spread_done = [splat(done, m) for m in range(G)]
        solved = []
        for j in range(G):
            total = None
            for m in range(j, G):
                term = inv[m, j] * spread_done[m]
                total = term if total is None else total + term
            solved.append(total)
        for h in range(g + 1, n):
            old = groups[h]
            new = jnp.where(inside, 0.0, old)
            for m in range(G):
                c = jnp.broadcast_to(old[:, base + m:base + m + 1], (G, B))
                new = new - c * solved[m]
            groups[h] = new
    return out

def chol_inverse_kernel(a_ref, o_ref, t_ref, d_ref):
    t_ref[...] = a_ref[...]
    row = lax.broadcasted_iota(jnp.int32, (W, B), 0)
    eye = jnp.where(lax.broadcasted_iota(jnp.int32, (B, B), 0) == lax.broadcasted_iota(jnp.int32, (B, B), 1), 1.0, 0.0).astype(jnp.float32)
    lane_w = lax.broadcasted_iota(jnp.int32, (B, W), 1)

    def step(b, carry):
        here = pl.ds(pl.multiple_of(b * B, B), B)
        panel = t_ref[:, here]
        block = t_ref[here, here]
        groups = [block[g * G:(g + 1) * G, :] for g in range(B // G)]
        inv = factor_block(groups)
        for g in range(B // G):
            d_ref[g * G:(g + 1) * G, :] = inv[g]
        inverse = d_ref[...]
        t_ref[here, here] = eye
        done = jnp.dot(inverse, t_ref[here, :], precision=HI, preferred_element_type=jnp.float32)
        coef = lax.dot_general(panel, inverse, (((1,), (1,)), ((), ())), precision=HI, preferred_element_type=jnp.float32)
        coef = jnp.where(row >= (b + 1) * B, coef, 0.0)
        t_ref[:, here] = jnp.where(row >= b * B, 0.0, panel)
        t_ref[...] = t_ref[...] - jnp.dot(coef, done, precision=HI, preferred_element_type=jnp.float32)
        t_ref[here, :] = jnp.where(lane_w < (b + 1) * B, done, 0.0)
        return carry

    lax.fori_loop(0, W // B, step, 0)
    o_ref[...] = t_ref[...]

def chol_inverse(a):
    return pl.pallas_call(
        chol_inverse_kernel,
        out_shape=jax.ShapeDtypeStruct((W, W), jnp.float32),
        in_specs=[pl.BlockSpec(memory_space=pltpu.VMEM)],
        out_specs=pl.BlockSpec(memory_space=pltpu.VMEM),
        scratch_shapes=[pltpu.VMEM((W, W), jnp.float32), pltpu.VMEM((B, B), jnp.float32)],
        name="factor_inverse",
    )(a)


BF, F32 = jnp.bfloat16, jnp.float32


def halves(value):
    high = value.astype(BF)
    return high, (value - high.astype(F32)).astype(BF)


def product(left_high, left_low, right_high, right_low):
    return (
        jnp.dot(left_high, right_high, preferred_element_type=F32)
        + jnp.dot(left_high, right_low, preferred_element_type=F32)
        + jnp.dot(left_low, right_high, preferred_element_type=F32)
    )


def split_factor(inverse_ref, high_ref, low_ref):
    high, low = halves(inverse_ref[...])
    high_ref[...] = high
    low_ref[...] = low


def own_kernel(inverse_ref, panel_ref, left_ref, slice_ref, lh, ll, ph, pq, xt):
    split_factor(inverse_ref, lh, ll)
    high, low = halves(panel_ref[...])
    ph[...] = high
    pq[...] = low
    rows = panel_ref.shape[1]
    for top in range(0, W, 2 * B):
        depth = top + 2 * B
        for first in range(0, rows, 2 * B):
            cut = slice(first, first + 2 * B)
            xt[top:depth, cut] = product(
                lh[top:depth, :depth], ll[top:depth, :depth], ph[:depth, cut], pq[:depth, cut]
            )
    mine = slice_ref.shape[0]
    start = pl.multiple_of(lax.axis_index("col") * mine, mine)
    slice_ref[...] = xt[pl.ds(start, mine), :]
    for block in range(rows // B):
        for part in range(W // B):
            turned = xt[part * B:(part + 1) * B, block * B:(block + 1) * B].T
            high, low = halves(turned)
            left_ref[block, :B, part * B:(part + 1) * B] = high
            left_ref[block, B:, part * B:(part + 1) * B] = low


def tile_step(targets_ref, left_ref, right, tiles_ref, out_ref, side, blocks, groups):
    def one(slot, carry):
        p = targets_ref[0, slot]
        q = targets_ref[1, slot]
        group = lax.rem(lax.div(lax.div(q, blocks), lax.axis_size("col")), groups)
        which = jnp.where(group == side, 0, 1) * blocks + lax.rem(q, blocks)
        four = jnp.dot(left_ref[lax.rem(p, blocks)], right[which], preferred_element_type=F32)
        update = four[:B, :B] + (four[:B, B:] + four[B:, :B])
        tile = tiles_ref[slot]
        out_ref[slot] = jnp.where(p >= q, tile - update, tile)
        return carry

    lax.fori_loop(0, out_ref.shape[0], one, 0)


def tiles_kernel(targets_ref, inverse_ref, left_ref, far_ref, tiles_ref, out_ref, lh, ll, ph, pq, right):
    split_factor(inverse_ref, lh, ll)
    blocks = left_ref.shape[0]
    size = far_ref.shape[2]
    side = lax.div(lax.axis_index("row"), lax.axis_size("col"))
    for slot in range(2):
        for k in range(W // size):
            high, low = halves(far_ref[k, slot])
            ph[k * size:(k + 1) * size, :] = high
            pq[k * size:(k + 1) * size, :] = low

        def columns(step, carry):
            cut = pl.ds(pl.multiple_of(step * 2 * B, 2 * B), 2 * B)
            for top in range(0, W, 2 * B):
                depth = top + 2 * B
                both = product(lh[top:depth, :depth], ll[top:depth, :depth], ph[:depth, cut], pq[:depth, cut])
                high, low = halves(both)
                for part in range(2):
                    at = slot * blocks + step * 2 + part
                    right[at, top:depth, :B] = high[:, part * B:(part + 1) * B]
                    right[at, top:depth, B:] = low[:, part * B:(part + 1) * B]
            return carry

        lax.fori_loop(0, blocks // 2, columns, 0)
    tile_step(targets_ref, left_ref, right, tiles_ref, out_ref, side, blocks, 2)


def vmem(count):
    return [pl.BlockSpec(memory_space=pltpu.VMEM)] * count


def on_device(diag_block, panel, tiles, targets):
    n_rows, n_cols = lax.axis_size("row"), lax.axis_size("col")
    size, rows = panel.shape[1], panel.shape[0]
    blocks = rows // B
    mine = panel.T
    own = lax.all_gather(mine, "col", axis=0, tiled=True)
    at = lambda r, c: r * n_cols + c
    first, second = [], []
    for r in range(n_rows):
        for c in range(n_cols):
            if r < n_cols:
                first.append((at(r, c), at(c, r)))
                second.append((at(r, c), at(c + n_cols, r)))
            else:
                first.append((at(r, c), at(c + n_cols, r - n_cols)))
    near = lax.ppermute(mine, ("row", "col"), first)
    other = lax.ppermute(mine, ("row", "col"), second)
    lines = [[side * n_cols + z for z in range(n_cols)] for side in range(n_rows // n_cols)]
    far = lax.all_gather(jnp.stack([near, other]), "row", axis=0, axis_index_groups=lines)
    inverse = chol_inverse(diag_block)
    factor = [pltpu.VMEM((W, W), BF)] * 2
    piece = [pltpu.VMEM((W, rows), BF)] * 2
    left, panel_slice = pl.pallas_call(
        own_kernel,
        out_shape=(
            jax.ShapeDtypeStruct((blocks, 2 * B, W), BF),
            jax.ShapeDtypeStruct((size, rows), F32),
        ),
        in_specs=vmem(2),
        out_specs=tuple(vmem(2)),
        scratch_shapes=[*factor, *piece, pltpu.VMEM((W, rows), F32)],
        name="own_rows",
    )(inverse, own)
    schur = pl.pallas_call(
        tiles_kernel,
        out_shape=jax.ShapeDtypeStruct(tiles.shape, F32),
        in_specs=[pl.BlockSpec(memory_space=pltpu.SMEM), *vmem(4)],
        out_specs=vmem(1)[0],
        scratch_shapes=[*factor, *piece, pltpu.VMEM((2 * blocks, W, 2 * B), BF)],
        name="schur_tiles",
    )(targets.T, inverse, left, far, tiles)
    return panel_slice.T, schur


def solution(mesh):
    placed = (P(), P("row", "col"), P(("row", "col"), None, None), P(("row", "col"), None))
    return jax.shard_map(
        on_device,
        mesh=mesh,
        in_specs=placed,
        out_specs=(P("row", "col"), P(("row", "col"), None, None)),
        check_vma=False,
    )
```

```python
import jax
import jax.numpy as jnp
from jax import lax
from jax.experimental import pallas as pl
from jax.experimental.pallas import tpu as pltpu
from jax.sharding import PartitionSpec as P

W, B, G, UNROLL = 512, 128, 8, 4
HI = lax.Precision.HIGHEST

def splat(col, k):
    return jnp.broadcast_to(col[k:k + 1, :], (G, B))

def factor_block(groups):
    n = len(groups)
    lane = lax.broadcasted_iota(jnp.int32, (G, B), 1)
    sub = lax.broadcasted_iota(jnp.int32, (G, B), 0)
    out = []
    for g in range(n):
        base = g * G
        rows = groups[g]
        cols = [jnp.broadcast_to(rows[:, base + m:base + m + 1], (G, B)) for m in range(G)]
        a = {(k, m): splat(cols[m], k) for m in range(G) for k in range(m, G)}
        inv = {}
        low = {}
        for m in range(G):
            r = lax.rsqrt(a[m, m])
            inv[m, m] = r
            for k in range(m + 1, G):
                low[k, m] = a[k, m] * r
            for j in range(m + 1, G):
                for k in range(j, G):
                    a[k, j] = a[k, j] - low[k, m] * low[j, m]
            for j in range(m):
                total = low[m, j] * inv[j, j]
                for k in range(j + 1, m):
                    total = total + low[m, k] * inv[k, j]
                inv[m, j] = -total * r
        inside = (lane >= base) & (lane < base + G)
        unit = jnp.where(lane - base == sub, 1.0, 0.0).astype(jnp.float32)
        rows = jnp.where(inside, unit, rows)
        spread = [splat(rows, m) for m in range(G)]
        done = None
        for m in range(G):
            column = inv[m, m]
            for k in range(m + 1, G):
                column = jnp.where(sub == k, inv[k, m], column)
            column = jnp.where(sub < m, 0.0, column)
            term = column * spread[m]
            done = term if done is None else done + term
        out.append(jnp.where(lane < base + G, done, 0.0))
        if g + 1 == n:
            break
        spread_done = [splat(done, m) for m in range(G)]
        solved = []
        for j in range(G):
            total = None
            for m in range(j, G):
                term = inv[m, j] * spread_done[m]
                total = term if total is None else total + term
            solved.append(total)
        for h in range(g + 1, n):
            old = groups[h]
            new = jnp.where(inside, 0.0, old)
            for m in range(G):
                c = jnp.broadcast_to(old[:, base + m:base + m + 1], (G, B))
                new = new - c * solved[m]
            groups[h] = new
    return out

def chol_inverse_kernel(a_ref, o_ref, t_ref, d_ref):
    t_ref[...] = a_ref[...]
    row = lax.broadcasted_iota(jnp.int32, (W, B), 0)
    eye = jnp.where(lax.broadcasted_iota(jnp.int32, (B, B), 0) == lax.broadcasted_iota(jnp.int32, (B, B), 1), 1.0, 0.0).astype(jnp.float32)
    lane_w = lax.broadcasted_iota(jnp.int32, (B, W), 1)

    def step(b, carry):
        here = pl.ds(pl.multiple_of(b * B, B), B)
        panel = t_ref[:, here]
        block = t_ref[here, here]
        groups = [block[g * G:(g + 1) * G, :] for g in range(B // G)]
        inv = factor_block(groups)
        for g in range(B // G):
            d_ref[g * G:(g + 1) * G, :] = inv[g]
        inverse = d_ref[...]
        t_ref[here, here] = eye
        done = jnp.dot(inverse, t_ref[here, :], precision=HI, preferred_element_type=jnp.float32)
        coef = lax.dot_general(panel, inverse, (((1,), (1,)), ((), ())), precision=HI, preferred_element_type=jnp.float32)
        coef = jnp.where(row >= (b + 1) * B, coef, 0.0)
        t_ref[:, here] = jnp.where(row >= b * B, 0.0, panel)
        t_ref[...] = t_ref[...] - jnp.dot(coef, done, precision=HI, preferred_element_type=jnp.float32)
        t_ref[here, :] = jnp.where(lane_w < (b + 1) * B, done, 0.0)
        return carry

    lax.fori_loop(0, W // B, step, 0)
    o_ref[...] = t_ref[...]

def chol_inverse(a):
    return pl.pallas_call(
        chol_inverse_kernel,
        out_shape=jax.ShapeDtypeStruct((W, W), jnp.float32),
        in_specs=[pl.BlockSpec(memory_space=pltpu.VMEM)],
        out_specs=pl.BlockSpec(memory_space=pltpu.VMEM),
        scratch_shapes=[pltpu.VMEM((W, W), jnp.float32), pltpu.VMEM((B, B), jnp.float32)],
        name="factor_inverse",
    )(a)


BF, F32 = jnp.bfloat16, jnp.float32


def halves(value):
    high = value.astype(BF)
    return high, (value - high.astype(F32)).astype(BF)


def product(left_high, left_low, right_high, right_low):
    return (
        jnp.dot(left_high, right_high, preferred_element_type=F32)
        + jnp.dot(left_high, right_low, preferred_element_type=F32)
        + jnp.dot(left_low, right_high, preferred_element_type=F32)
    )


def split_factor(inverse_ref, high_ref, low_ref):
    high, low = halves(inverse_ref[...])
    high_ref[...] = high
    low_ref[...] = low


def own_kernel(inverse_ref, panel_ref, partner_ref, left_ref, slice_ref, lh, ll, ph, pq, xh, xl, xt):
    split_factor(inverse_ref, lh, ll)
    size = slice_ref.shape[0]
    col = lax.axis_index("col")
    for j, flip in enumerate(gathered_order(W // size)):
        to = pl.ds(pl.multiple_of(jnp.bitwise_xor(col, flip) * size, size), size)
        at = j * size % (W // 2)
        source = panel_ref if j * size < W // 2 else partner_ref
        high, low = halves(source[at:at + size, :])
        ph[to, :] = high
        pq[to, :] = low
    rows = panel_ref.shape[1]
    for top in range(0, W, 2 * B):
        depth = top + 2 * B
        for first in range(0, rows, 2 * B):
            cut = slice(first, first + 2 * B)
            xt[top:depth, cut] = product(
                lh[top:depth, :depth], ll[top:depth, :depth], ph[:depth, cut], pq[:depth, cut]
            )
    slice_ref[...] = xt[pl.ds(pl.multiple_of(col * size, size), size), :]
    for first in range(0, rows, B):
        for part in range(0, W, B):
            high, low = halves(xt[part:part + B, first:first + B].T)
            xh[first:first + B, part:part + B] = high
            xl[first:first + B, part:part + B] = low
    for first in range(0, rows, 2 * B):
        cut = slice(first, first + 2 * B)
        for top in range(0, W, 2 * B):
            across = slice(top, top + 2 * B)
            high, low = halves(product(xh[cut, top:], xl[cut, top:], lh[top:, across], ll[top:, across]))
            for part in range(2):
                left_ref[first // B + part, :B, across] = high[part * B:(part + 1) * B]
                left_ref[first // B + part, B:, across] = low[part * B:(part + 1) * B]


def tiles_kernel(targets_ref, left_hbm, far_hbm, tiles_hbm, out_hbm, left, far, tiles, out, right, in_sem, far_sem, out_sem):
    blocks, size, planes = left.shape[0], far.shape[2], far.shape[0]
    count = out.shape[0]
    col, row = lax.axis_index("col"), lax.axis_index("row")
    n_cols = lax.axis_size("col")
    side = lax.div(row, n_cols)
    far_copies = [pltpu.make_async_copy(far_hbm.at[z], far.at[z], far_sem.at[z]) for z in range(planes)]
    left_copy = pltpu.make_async_copy(left_hbm, left, in_sem.at[0])
    tiles_copy = pltpu.make_async_copy(tiles_hbm, tiles, in_sem.at[1])
    for copy in far_copies:
        copy.start()
    left_copy.start()
    tiles_copy.start()
    for z in range(planes):
        far_copies[z].wait()
        apart = lax.rem(z - col + n_cols, n_cols)
        k = jnp.where(apart < planes // 2, 2 * apart, 2 * planes - 1 - 2 * apart)
        to = pl.ds(pl.multiple_of(k * size, size), size)
        for slot in range(2):
            high, low = halves(far[z, slot])
            for block in range(blocks):
                right[slot * blocks + block, to, :B] = high[:, block * B:(block + 1) * B]
                right[slot * blocks + block, to, B:] = low[:, block * B:(block + 1) * B]
    left_copy.wait()
    tiles_copy.wait()

    def one(slot, carry):
        p = targets_ref[0, slot]
        q = targets_ref[1, slot]
        group = lax.rem(lax.div(lax.div(q, blocks), n_cols), 2)
        which = jnp.where(group == side, 0, 1) * blocks + lax.rem(q, blocks)
        four = jnp.dot(left[lax.rem(p, blocks)], right[which], preferred_element_type=F32)
        update = four[:B, :B] + (four[:B, B:] + four[B:, :B])
        tile = tiles[slot]
        out[slot] = jnp.where(p >= q, tile - update, tile)
        pltpu.make_async_copy(out.at[slot], out_hbm.at[slot], out_sem.at[slot]).start()
        return carry

    lax.fori_loop(0, count, one, 0, unroll=UNROLL)

    def drain(slot, carry):
        pltpu.make_async_copy(out.at[slot], out_hbm.at[slot], out_sem.at[slot]).wait()
        return carry

    lax.fori_loop(0, count, drain, 0)


def vmem(count):
    return [pl.BlockSpec(memory_space=pltpu.VMEM)] * count


def gathered_order(n_cols):
    order = [0]
    for flip in (n_cols // 4, n_cols // 8, n_cols // 2, 1):
        order += [entry ^ flip for entry in order]
    return order


def on_device(diag_block, panel, tiles, targets):
    n_rows, n_cols = lax.axis_size("row"), lax.axis_size("col")
    size, rows = panel.shape[1], panel.shape[0]
    blocks, count = rows // B, tiles.shape[0]
    mine = panel.T

    def at(r, c):
        return r * n_cols + c

    def shifted(r, c):
        step = c // 2 if c % 2 == 0 else n_cols - 1 - c // 2
        return r // n_cols * n_cols + (r + step) % n_cols

    turn = [(at(r, c), at(shifted(r, c), r % n_cols)) for r in range(n_rows) for c in range(n_cols)]
    lift = [(at(r, c), at(r + n_cols, c)) for r in range(n_cols) for c in range(n_cols)]
    near = lax.ppermute(mine, ("row", "col"), turn)
    other = lax.ppermute(near, ("row", "col"), lift)
    lines = [[part * n_cols + z for z in range(n_cols)] for part in range(n_rows // n_cols)]
    far = lax.all_gather(jnp.stack([near, other]), "row", axis=0, axis_index_groups=lines)

    own, diag, _ = lax.optimization_barrier((mine, diag_block, other))
    for flip in (n_cols // 4, n_cols // 8, n_cols // 2, 1):
        pairs = [(c, c ^ flip) for c in range(n_cols)]
        received = lax.ppermute(own, "col", pairs)
        if flip != 1:
            own = jnp.concatenate([own, received])
    inverse = chol_inverse(diag)
    any_space = pl.BlockSpec(memory_space=pl.ANY)
    left, panel_slice = pl.pallas_call(
        own_kernel,
        out_shape=(
            jax.ShapeDtypeStruct((blocks, 2 * B, W), BF),
            jax.ShapeDtypeStruct((size, rows), F32),
        ),
        in_specs=vmem(3),
        out_specs=tuple(vmem(2)),
        scratch_shapes=[
            *[pltpu.VMEM((W, W), BF)] * 2,
            *[pltpu.VMEM((W, rows), BF)] * 2,
            *[pltpu.VMEM((rows, W), BF)] * 2,
            pltpu.VMEM((W, rows), F32),
        ],
        name="own_rows",
    )(inverse, own, received)
    schur = pl.pallas_call(
        tiles_kernel,
        out_shape=jax.ShapeDtypeStruct(tiles.shape, F32),
        in_specs=[pl.BlockSpec(memory_space=pltpu.SMEM), *[any_space] * 3],
        out_specs=any_space,
        scratch_shapes=[
            pltpu.VMEM(left.shape, BF),
            pltpu.VMEM(far.shape, F32),
            pltpu.VMEM(tiles.shape, F32),
            pltpu.VMEM(tiles.shape, F32),
            pltpu.VMEM((2 * blocks, W, 2 * B), BF),
            pltpu.SemaphoreType.DMA((2,)),
            pltpu.SemaphoreType.DMA((far.shape[0],)),
            pltpu.SemaphoreType.DMA((count,)),
        ],
        name="schur_tiles",
    )(targets.T, left, far, tiles)
    return panel_slice.T, schur


def solution(mesh):
    placed = (P(), P("row", "col"), P(("row", "col"), None, None), P(("row", "col"), None))
    return jax.shard_map(
        on_device,
        mesh=mesh,
        in_specs=placed,
        out_specs=(P("row", "col"), P(("row", "col"), None, None)),
        check_vma=False,
    )
```

```python
import functools

import jax
import jax.numpy as jnp
from jax import lax
from jax.experimental import pallas as pl
from jax.experimental.pallas import tpu as pltpu
from jax.sharding import PartitionSpec as P

W, B, G, UNROLL = 512, 128, 8, 4
HI = lax.Precision.HIGHEST

def splat(col, k):
    return jnp.broadcast_to(col[k:k + 1, :], (G, B))

def factor_block(groups):
    n = len(groups)
    lane = lax.broadcasted_iota(jnp.int32, (G, B), 1)
    sub = lax.broadcasted_iota(jnp.int32, (G, B), 0)
    out = []
    for g in range(n):
        base = g * G
        rows = groups[g]
        cols = [jnp.broadcast_to(rows[:, base + m:base + m + 1], (G, B)) for m in range(G)]
        a = {(k, m): splat(cols[m], k) for m in range(G) for k in range(m, G)}
        inv = {}
        low = {}
        for m in range(G):
            r = lax.rsqrt(a[m, m])
            inv[m, m] = r
            for k in range(m + 1, G):
                low[k, m] = a[k, m] * r
            for j in range(m + 1, G):
                for k in range(j, G):
                    a[k, j] = a[k, j] - low[k, m] * low[j, m]
            for j in range(m):
                total = low[m, j] * inv[j, j]
                for k in range(j + 1, m):
                    total = total + low[m, k] * inv[k, j]
                inv[m, j] = -total * r
        inside = (lane >= base) & (lane < base + G)
        unit = jnp.where(lane - base == sub, 1.0, 0.0).astype(jnp.float32)
        rows = jnp.where(inside, unit, rows)
        spread = [splat(rows, m) for m in range(G)]
        done = None
        for m in range(G):
            column = inv[m, m]
            for k in range(m + 1, G):
                column = jnp.where(sub == k, inv[k, m], column)
            column = jnp.where(sub < m, 0.0, column)
            term = column * spread[m]
            done = term if done is None else done + term
        out.append(jnp.where(lane < base + G, done, 0.0))
        if g + 1 == n:
            break
        spread_done = [splat(done, m) for m in range(G)]
        solved = []
        for j in range(G):
            total = None
            for m in range(j, G):
                term = inv[m, j] * spread_done[m]
                total = term if total is None else total + term
            solved.append(total)
        for h in range(g + 1, n):
            old = groups[h]
            new = jnp.where(inside, 0.0, old)
            for m in range(G):
                c = jnp.broadcast_to(old[:, base + m:base + m + 1], (G, B))
                new = new - c * solved[m]
            groups[h] = new
    return out

def dot(left, right):
    return jnp.dot(left, right, precision=HI, preferred_element_type=jnp.float32)


def factor_step_kernel(b, a_ref, o_ref, d_ref):
    start, end = b * B, (b + 1) * B
    block = a_ref[start:end, start:end]
    for g, rows in enumerate(factor_block([block[g * G:(g + 1) * G, :] for g in range(B // G)])):
        d_ref[g * G:(g + 1) * G, :] = rows
    inverse = d_ref[...]
    if b > 0:
        o_ref[:start, :] = a_ref[:start, :]
        before = dot(inverse, a_ref[start:end, :start])
        o_ref[start:end, :start] = before
    o_ref[start:end, start:end] = inverse
    if end < W:
        o_ref[start:end, end:] = jnp.zeros((B, W - end), jnp.float32)
        behind = dot(inverse, a_ref[start:end, end:])
        coef = lax.dot_general(
            a_ref[end:, start:end], inverse, (((1,), (1,)), ((), ())), precision=HI, preferred_element_type=jnp.float32
        )
        if b > 0:
            o_ref[end:, :start] = a_ref[end:, :start] - dot(coef, before)
        o_ref[end:, start:end] = -dot(coef, inverse)
        o_ref[end:, end:] = a_ref[end:, end:] - dot(coef, behind)


def factor_step(b, a):
    return pl.pallas_call(
        functools.partial(factor_step_kernel, b),
        out_shape=jax.ShapeDtypeStruct((W, W), jnp.float32),
        in_specs=[pl.BlockSpec(memory_space=pltpu.VMEM)],
        out_specs=pl.BlockSpec(memory_space=pltpu.VMEM),
        scratch_shapes=[pltpu.VMEM((B, B), jnp.float32)],
        name="factor_step",
    )(a)


BF, F32 = jnp.bfloat16, jnp.float32


def halves(value):
    high = value.astype(BF)
    return high, (value - high.astype(F32)).astype(BF)


def product(left_high, left_low, right_high, right_low):
    return (
        jnp.dot(left_high, right_high, preferred_element_type=F32)
        + jnp.dot(left_high, right_low, preferred_element_type=F32)
        + jnp.dot(left_low, right_high, preferred_element_type=F32)
    )


def split_factor(inverse_ref, high_ref, low_ref):
    high, low = halves(inverse_ref[...])
    high_ref[...] = high
    low_ref[...] = low


def own_kernel(inverse_ref, panel_ref, partner_ref, left_ref, slice_ref, lh, ll, ph, pq, xh, xl, xt):
    split_factor(inverse_ref, lh, ll)
    size = slice_ref.shape[0]
    col = lax.axis_index("col")
    for j, flip in enumerate(gathered_order(W // size)):
        to = pl.ds(pl.multiple_of(jnp.bitwise_xor(col, flip) * size, size), size)
        at = j * size % (W // 2)
        source = panel_ref if j * size < W // 2 else partner_ref
        high, low = halves(source[at:at + size, :])
        ph[to, :] = high
        pq[to, :] = low
    rows = panel_ref.shape[1]
    for top in range(0, W, 2 * B):
        depth = top + 2 * B
        for first in range(0, rows, 2 * B):
            cut = slice(first, first + 2 * B)
            xt[top:depth, cut] = product(
                lh[top:depth, :depth], ll[top:depth, :depth], ph[:depth, cut], pq[:depth, cut]
            )
    slice_ref[...] = xt[pl.ds(pl.multiple_of(col * size, size), size), :]
    for first in range(0, rows, B):
        for part in range(0, W, B):
            high, low = halves(xt[part:part + B, first:first + B].T)
            xh[first:first + B, part:part + B] = high
            xl[first:first + B, part:part + B] = low
    for first in range(0, rows, 2 * B):
        cut = slice(first, first + 2 * B)
        for top in range(0, W, 2 * B):
            across = slice(top, top + 2 * B)
            high, low = halves(product(xh[cut, top:], xl[cut, top:], lh[top:, across], ll[top:, across]))
            for part in range(2):
                left_ref[first // B + part, :B, across] = high[part * B:(part + 1) * B]
                left_ref[first // B + part, B:, across] = low[part * B:(part + 1) * B]


def tiles_kernel(reach, targets_ref, left_hbm, tiles_hbm, *refs):
    pieces, (out_hbm, left, far, tiles, out, right, in_sem, far_sem, out_sem) = refs[:len(reach)], refs[len(reach):]
    blocks, size = left.shape[0], far.shape[2]
    count = out.shape[0]
    col, row = lax.axis_index("col"), lax.axis_index("row")
    n_cols = lax.axis_size("col")
    side = lax.div(row, n_cols)
    far_copies = [pltpu.make_async_copy(piece, far.at[i], far_sem.at[i]) for i, piece in enumerate(pieces)]
    left_copy = pltpu.make_async_copy(left_hbm, left, in_sem.at[0])
    tiles_copy = pltpu.make_async_copy(tiles_hbm, tiles, in_sem.at[1])
    for copy in far_copies:
        copy.start()
    left_copy.start()
    tiles_copy.start()
    for i, away in enumerate(reach):
        far_copies[i].wait()
        for part in range(far.shape[1]):
            twin, slot = part % 2, part // 2
            apart = lax.rem(row + away - col - twin * (n_cols // 2) + 4 * n_cols, n_cols)
            k = jnp.where(apart < n_cols // 2, 2 * apart, 2 * n_cols - 1 - 2 * apart)
            to = pl.ds(pl.multiple_of(k * size, size), size)
            high, low = halves(far[i, part])
            for block in range(blocks):
                right[slot * blocks + block, to, :B] = high[:, block * B:(block + 1) * B]
                right[slot * blocks + block, to, B:] = low[:, block * B:(block + 1) * B]
    left_copy.wait()
    tiles_copy.wait()

    def one(slot, carry):
        p = targets_ref[0, slot]
        q = targets_ref[1, slot]
        group = lax.rem(lax.div(lax.div(q, blocks), n_cols), 2)
        which = jnp.where(group == side, 0, 1) * blocks + lax.rem(q, blocks)
        four = jnp.dot(left[lax.rem(p, blocks)], right[which], preferred_element_type=F32)
        update = four[:B, :B] + (four[:B, B:] + four[B:, :B])
        tile = tiles[slot]
        out[slot] = jnp.where(p >= q, tile - update, tile)
        pltpu.make_async_copy(out.at[slot], out_hbm.at[slot], out_sem.at[slot]).start()
        return carry

    lax.fori_loop(0, count, one, 0, unroll=UNROLL)

    def drain(slot, carry):
        pltpu.make_async_copy(out.at[slot], out_hbm.at[slot], out_sem.at[slot]).wait()
        return carry

    lax.fori_loop(0, count, drain, 0)


def vmem(count):
    return [pl.BlockSpec(memory_space=pltpu.VMEM)] * count


def gathered_order(n_cols):
    order = [0]
    for flip in (n_cols // 4, n_cols // 8, n_cols // 2, 1):
        order += [entry ^ flip for entry in order]
    return order


def on_device(diag_block, panel, tiles, targets):
    n_rows, n_cols = lax.axis_size("row"), lax.axis_size("col")
    size, rows = panel.shape[1], panel.shape[0]
    blocks, count = rows // B, tiles.shape[0]
    mine = panel.T
    half = n_cols // 2
    together = lax.optimization_barrier

    def at(r, c):
        return r * n_cols + c

    def moved(r, step):
        return r // n_cols * n_cols + (r + step) % n_cols

    def spread(c):
        return c // 2 if c % 2 == 0 else n_cols - 1 - c // 2

    everyone = [(r, c) for r in range(n_rows) for c in range(n_cols)]
    turn = [(at(r, c), at(moved(r, spread(c)), r % n_cols)) for r, c in everyone]
    twin = [(at(r, c), at(moved(r, spread(c) + half), r % n_cols)) for r, c in everyone]
    lift = [(at(r, c), at(r + n_cols, c)) for r, c in everyone if r < n_cols]
    up = [(r, moved(r, 1)) for r in range(n_rows)]
    down = [(r, moved(r, -1)) for r in range(n_rows)]
    flips = [[(c, c ^ flip) for c in range(n_cols)] for flip in (n_cols // 4, n_cols // 8, n_cols // 2, 1)]

    first = lax.ppermute(mine, ("row", "col"), turn)
    second = lax.ppermute(mine, ("row", "col"), twin)
    work = factor_step(0, diag_block)
    first, second, work, own = together((first, second, work, mine))

    near = jnp.stack([first, second])
    other = lax.ppermute(near, ("row", "col"), lift)
    received = lax.ppermute(own, "col", flips[0])
    work = factor_step(1, work)
    near, other, received, work = together((near, other, received, work))

    base = jnp.concatenate([near, other])
    own = jnp.concatenate([own, received])
    upward, downward, pieces, reach = base, base, [base], [0]
    for step in range(1, half // 2 + 1):
        upward = lax.ppermute(upward, "row", up)
        pieces.append(upward)
        reach.append(-step)
        if step < half // 2:
            downward = lax.ppermute(downward, "row", down)
            pieces.append(downward)
            reach.append(step)
        if step < len(flips):
            received = lax.ppermute(own, "col", flips[step])
        if step + 1 < W // B:
            work = factor_step(step + 1, work)
        upward, downward, received, work, own = together((upward, downward, received, work, own))
        pieces[-1 if step == half // 2 else -2] = upward
        if step < half // 2:
            pieces[-1] = downward
        if step + 1 < len(flips):
            own = jnp.concatenate([own, received])
        if step + 1 == len(flips):
            left, panel_slice = own_rows(work, own, received, size, blocks)
    any_space = pl.BlockSpec(memory_space=pl.ANY)
    schur = pl.pallas_call(
        functools.partial(tiles_kernel, tuple(reach)),
        out_shape=jax.ShapeDtypeStruct(tiles.shape, F32),
        in_specs=[pl.BlockSpec(memory_space=pltpu.SMEM), *[any_space] * (2 + len(pieces))],
        out_specs=any_space,
        scratch_shapes=[
            pltpu.VMEM(left.shape, BF),
            pltpu.VMEM((len(pieces), *base.shape), F32),
            pltpu.VMEM(tiles.shape, F32),
            pltpu.VMEM(tiles.shape, F32),
            pltpu.VMEM((2 * blocks, W, 2 * B), BF),
            pltpu.SemaphoreType.DMA((2,)),
            pltpu.SemaphoreType.DMA((len(pieces),)),
            pltpu.SemaphoreType.DMA((count,)),
        ],
        name="schur_tiles",
    )(targets.T, left, tiles, *pieces)
    return panel_slice.T, schur


def own_rows(inverse, own, received, size, blocks):
    rows = own.shape[1]
    return pl.pallas_call(
        own_kernel,
        out_shape=(
            jax.ShapeDtypeStruct((blocks, 2 * B, W), BF),
            jax.ShapeDtypeStruct((size, rows), F32),
        ),
        in_specs=vmem(3),
        out_specs=tuple(vmem(2)),
        scratch_shapes=[
            *[pltpu.VMEM((W, W), BF)] * 2,
            *[pltpu.VMEM((W, rows), BF)] * 2,
            *[pltpu.VMEM((rows, W), BF)] * 2,
            pltpu.VMEM((W, rows), F32),
        ],
        name="own_rows",
    )(inverse, own, received)


def solution(mesh):
    placed = (P(), P("row", "col"), P(("row", "col"), None, None), P(("row", "col"), None))
    return jax.shard_map(
        on_device,
        mesh=mesh,
        in_specs=placed,
        out_specs=(P("row", "col"), P(("row", "col"), None, None)),
        check_vma=False,
    )
```

```python
import functools

import jax
import jax.numpy as jnp
from jax import lax
from jax.experimental import pallas as pl
from jax.experimental.pallas import tpu as pltpu
from jax.sharding import PartitionSpec as P

W, B, G, UNROLL = 512, 128, 8, 4
HI = lax.Precision.HIGHEST


def splat(col, k):
    return jnp.broadcast_to(col[k:k + 1, :], (G, B))


def factor_block(groups):
    n = len(groups)
    lane = lax.broadcasted_iota(jnp.int32, (G, B), 1)
    sub = lax.broadcasted_iota(jnp.int32, (G, B), 0)
    out = []
    for g in range(n):
        base = g * G
        rows = groups[g]
        cols = [jnp.broadcast_to(rows[:, base + m:base + m + 1], (G, B)) for m in range(G)]
        a = {(k, m): splat(cols[m], k) for m in range(G) for k in range(m, G)}
        inv = {}
        low = {}
        for m in range(G):
            r = lax.rsqrt(a[m, m])
            inv[m, m] = r
            for k in range(m + 1, G):
                low[k, m] = a[k, m] * r
            for j in range(m + 1, G):
                for k in range(j, G):
                    a[k, j] = a[k, j] - low[k, m] * low[j, m]
            for j in range(m):
                total = low[m, j] * inv[j, j]
                for k in range(j + 1, m):
                    total = total + low[m, k] * inv[k, j]
                inv[m, j] = -total * r
        inside = (lane >= base) & (lane < base + G)
        unit = jnp.where(lane - base == sub, 1.0, 0.0).astype(jnp.float32)
        rows = jnp.where(inside, unit, rows)
        spread = [splat(rows, m) for m in range(G)]
        done = None
        for m in range(G):
            column = inv[m, m]
            for k in range(m + 1, G):
                column = jnp.where(sub == k, inv[k, m], column)
            column = jnp.where(sub < m, 0.0, column)
            term = column * spread[m]
            done = term if done is None else done + term
        out.append(jnp.where(lane < base + G, done, 0.0))
        if g + 1 == n:
            break
        spread_done = [splat(done, m) for m in range(G)]
        solved = []
        for j in range(G):
            total = None
            for m in range(j, G):
                term = inv[m, j] * spread_done[m]
                total = term if total is None else total + term
            solved.append(total)
        for h in range(g + 1, n):
            old = groups[h]
            new = jnp.where(inside, 0.0, old)
            for m in range(G):
                c = jnp.broadcast_to(old[:, base + m:base + m + 1], (G, B))
                new = new - c * solved[m]
            groups[h] = new
    return out


def dot(left, right):
    return jnp.dot(left, right, precision=HI, preferred_element_type=jnp.float32)


def factor_step_kernel(b, a_ref, o_ref, d_ref):
    start, end = b * B, (b + 1) * B
    block = a_ref[start:end, start:end]
    for g, rows in enumerate(factor_block([block[g * G:(g + 1) * G, :] for g in range(B // G)])):
        d_ref[g * G:(g + 1) * G, :] = rows
    inverse = d_ref[...]
    if b > 0:
        o_ref[:start, :] = a_ref[:start, :]
        before = dot(inverse, a_ref[start:end, :start])
        o_ref[start:end, :start] = before
    o_ref[start:end, start:end] = inverse
    if end < W:
        o_ref[start:end, end:] = jnp.zeros((B, W - end), jnp.float32)
        behind = dot(inverse, a_ref[start:end, end:])
        coef = lax.dot_general(
            a_ref[end:, start:end], inverse, (((1,), (1,)), ((), ())), precision=HI, preferred_element_type=jnp.float32
        )
        if b > 0:
            o_ref[end:, :start] = a_ref[end:, :start] - dot(coef, before)
        o_ref[end:, start:end] = -dot(coef, inverse)
        o_ref[end:, end:] = a_ref[end:, end:] - dot(coef, behind)


def factor_step(b, a):
    return pl.pallas_call(
        functools.partial(factor_step_kernel, b),
        out_shape=jax.ShapeDtypeStruct((W, W), jnp.float32),
        in_specs=[pl.BlockSpec(memory_space=pltpu.VMEM)],
        out_specs=pl.BlockSpec(memory_space=pltpu.VMEM),
        scratch_shapes=[pltpu.VMEM((B, B), jnp.float32)],
        name="factor_step",
    )(a)


BF, F32 = jnp.bfloat16, jnp.float32


def halves(value):
    high = value.astype(BF)
    return high, (value - high.astype(F32)).astype(BF)


def product(left_high, left_low, right_high, right_low):
    return (
        jnp.dot(left_high, right_high, preferred_element_type=F32)
        + jnp.dot(left_high, right_low, preferred_element_type=F32)
        + jnp.dot(left_low, right_high, preferred_element_type=F32)
    )


def split_factor(inverse_ref, high_ref, low_ref):
    high, low = halves(inverse_ref[...])
    high_ref[...] = high
    low_ref[...] = low


def own_kernel(inverse_ref, panel_ref, partner_ref, left_ref, slice_ref, lh, ll, ph, pq, xh, xl, xt):
    split_factor(inverse_ref, lh, ll)
    size = slice_ref.shape[0]
    col = lax.axis_index("col")
    for j, flip in enumerate(gathered_order(W // size)):
        to = pl.ds(pl.multiple_of(jnp.bitwise_xor(col, flip) * size, size), size)
        at = j * size % (W // 2)
        source = panel_ref if j * size < W // 2 else partner_ref
        high, low = halves(source[at:at + size, :])
        ph[to, :] = high
        pq[to, :] = low
    rows = panel_ref.shape[1]
    for top in range(0, W, 2 * B):
        depth = top + 2 * B
        for first in range(0, rows, 2 * B):
            cut = slice(first, first + 2 * B)
            xt[top:depth, cut] = product(
                lh[top:depth, :depth], ll[top:depth, :depth], ph[:depth, cut], pq[:depth, cut]
            )
    slice_ref[...] = xt[pl.ds(pl.multiple_of(col * size, size), size), :]
    for first in range(0, rows, B):
        for part in range(0, W, B):
            high, low = halves(xt[part:part + B, first:first + B].T)
            xh[first:first + B, part:part + B] = high
            xl[first:first + B, part:part + B] = low
    for first in range(0, rows, 2 * B):
        cut = slice(first, first + 2 * B)
        for top in range(0, W, 2 * B):
            across = slice(top, top + 2 * B)
            high, low = halves(product(xh[cut, top:], xl[cut, top:], lh[top:, across], ll[top:, across]))
            for part in range(2):
                left_ref[first // B + part, :B, across] = high[part * B:(part + 1) * B]
                left_ref[first // B + part, B:, across] = low[part * B:(part + 1) * B]


def tiles_kernel(reach, targets_ref, left_hbm, tiles_hbm, *refs):
    pieces, (out_hbm, left, far, tiles, out, right, in_sem, far_sem, out_sem) = refs[:len(reach)], refs[len(reach):]
    blocks, size = left.shape[0], far.shape[2]
    count = out.shape[0]
    col, row = lax.axis_index("col"), lax.axis_index("row")
    n_cols = lax.axis_size("col")
    side = lax.div(row, n_cols)
    far_copies = [pltpu.make_async_copy(piece, far.at[i], far_sem.at[i]) for i, piece in enumerate(pieces)]
    left_copy = pltpu.make_async_copy(left_hbm, left, in_sem.at[0])
    tiles_copy = pltpu.make_async_copy(tiles_hbm, tiles, in_sem.at[1])
    for copy in far_copies:
        copy.start()
    left_copy.start()
    tiles_copy.start()
    for i, away in enumerate(reach):
        far_copies[i].wait()
        for part in range(far.shape[1]):
            twin, slot = part % 2, part // 2
            apart = lax.rem(row + away - col - twin * (n_cols // 2) + 4 * n_cols, n_cols)
            k = jnp.where(apart < n_cols // 2, 2 * apart, 2 * n_cols - 1 - 2 * apart)
            to = pl.ds(pl.multiple_of(k * size, size), size)
            high, low = halves(far[i, part])
            for block in range(blocks):
                right[slot * blocks + block, to, :B] = high[:, block * B:(block + 1) * B]
                right[slot * blocks + block, to, B:] = low[:, block * B:(block + 1) * B]
    left_copy.wait()
    tiles_copy.wait()

    def one(slot, carry):
        p = targets_ref[0, slot]
        q = targets_ref[1, slot]
        group = lax.rem(lax.div(lax.div(q, blocks), n_cols), 2)
        which = jnp.where(group == side, 0, 1) * blocks + lax.rem(q, blocks)
        four = jnp.dot(left[lax.rem(p, blocks)], right[which], preferred_element_type=F32)
        update = four[:B, :B] + (four[:B, B:] + four[B:, :B])
        tile = tiles[slot]
        out[slot] = jnp.where(p >= q, tile - update, tile)
        pltpu.make_async_copy(out.at[slot], out_hbm.at[slot], out_sem.at[slot]).start()
        return carry

    lax.fori_loop(0, count, one, 0, unroll=UNROLL)

    def drain(slot, carry):
        pltpu.make_async_copy(out.at[slot], out_hbm.at[slot], out_sem.at[slot]).wait()
        return carry

    lax.fori_loop(0, count, drain, 0)


def vmem(count):
    return [pl.BlockSpec(memory_space=pltpu.VMEM)] * count


def gathered_order(n_cols):
    order = [0]
    for flip in (n_cols // 4, n_cols // 8, n_cols // 2, 1):
        order += [entry ^ flip for entry in order]
    return order


def on_device(diag_block, panel, tiles, targets):
    n_rows, n_cols = lax.axis_size("row"), lax.axis_size("col")
    size, rows = panel.shape[1], panel.shape[0]
    blocks, count = rows // B, tiles.shape[0]
    mine = panel.T
    half = n_cols // 2
    together = lax.optimization_barrier

    def at(r, c):
        return r * n_cols + c

    def moved(r, step):
        return r // n_cols * n_cols + (r + step) % n_cols

    def spread(c):
        return c // 2 if c % 2 == 0 else n_cols - 1 - c // 2

    everyone = [(r, c) for r in range(n_rows) for c in range(n_cols)]
    turn = [(at(r, c), at(moved(r, spread(c)), r % n_cols)) for r, c in everyone]
    twin = [(at(r, c), at(moved(r, spread(c) + half), r % n_cols)) for r, c in everyone]
    lift = [(at(r, c), at(r + n_cols, c)) for r, c in everyone if r < n_cols]
    up = [(r, moved(r, 1)) for r in range(n_rows)]
    down = [(r, moved(r, -1)) for r in range(n_rows)]
    flips = [[(c, c ^ flip) for c in range(n_cols)] for flip in (n_cols // 4, n_cols // 8, n_cols // 2, 1)]

    first = lax.ppermute(mine, ("row", "col"), turn)
    second = lax.ppermute(mine, ("row", "col"), twin)
    work = factor_step(0, diag_block)
    first, second, work, own = together((first, second, work, mine))

    near = jnp.stack([first, second])
    other = lax.ppermute(near, ("row", "col"), lift)
    received = lax.ppermute(own, "col", flips[0])
    near, other, work = together((near, other, work))

    base = jnp.concatenate([near, other])
    upward, downward, pieces, reach = base, base, [base], [0]
    for step in range(1, half // 2 + 1):
        both = step < half // 2
        upward = lax.ppermute(upward, "row", up)
        if both:
            downward = lax.ppermute(downward, "row", down)
        if step < W // B:
            work = factor_step(step, work)
            received, work = together((received, work))
            own = jnp.concatenate([own, received])
            received = lax.ppermute(own, "col", flips[step])
            if step + 1 == W // B:
                left, panel_slice = own_rows(work, own, received, size, blocks)
            upward, downward, work = together((upward, downward, work))
        else:
            upward, left, panel_slice = together((upward, left, panel_slice))
        pieces.append(upward)
        reach.append(-step)
        if both:
            pieces.append(downward)
            reach.append(step)
    any_space = pl.BlockSpec(memory_space=pl.ANY)
    schur = pl.pallas_call(
        functools.partial(tiles_kernel, tuple(reach)),
        out_shape=jax.ShapeDtypeStruct(tiles.shape, F32),
        in_specs=[pl.BlockSpec(memory_space=pltpu.SMEM), *[any_space] * (2 + len(pieces))],
        out_specs=any_space,
        scratch_shapes=[
            pltpu.VMEM(left.shape, BF),
            pltpu.VMEM((len(pieces), *base.shape), F32),
            pltpu.VMEM(tiles.shape, F32),
            pltpu.VMEM(tiles.shape, F32),
            pltpu.VMEM((2 * blocks, W, 2 * B), BF),
            pltpu.SemaphoreType.DMA((2,)),
            pltpu.SemaphoreType.DMA((len(pieces),)),
            pltpu.SemaphoreType.DMA((count,)),
        ],
        name="schur_tiles",
    )(targets.T, left, tiles, *pieces)
    return panel_slice.T, schur


def own_rows(inverse, own, received, size, blocks):
    rows = own.shape[1]
    return pl.pallas_call(
        own_kernel,
        out_shape=(
            jax.ShapeDtypeStruct((blocks, 2 * B, W), BF),
            jax.ShapeDtypeStruct((size, rows), F32),
        ),
        in_specs=vmem(3),
        out_specs=tuple(vmem(2)),
        scratch_shapes=[
            *[pltpu.VMEM((W, W), BF)] * 2,
            *[pltpu.VMEM((W, rows), BF)] * 2,
            *[pltpu.VMEM((rows, W), BF)] * 2,
            pltpu.VMEM((W, rows), F32),
        ],
        name="own_rows",
    )(inverse, own, received)


def solution(mesh):
    placed = (P(), P("row", "col"), P(("row", "col"), None, None), P(("row", "col"), None))
    return jax.shard_map(
        on_device,
        mesh=mesh,
        in_specs=placed,
        out_specs=(P("row", "col"), P(("row", "col"), None, None)),
        check_vma=False,
    )
```

```python
import functools

import jax
import jax.numpy as jnp
from jax import lax
from jax.experimental import pallas as pl
from jax.experimental.pallas import tpu as pltpu
from jax.sharding import PartitionSpec as P

W, B, G, UNROLL, COPIES = 512, 128, 8, 4, 4
HI = lax.Precision.HIGHEST


def splat(col, k):
    return jnp.broadcast_to(col[k:k + 1, :], (G, B))


def factor_block(groups):
    n = len(groups)
    lane = lax.broadcasted_iota(jnp.int32, (G, B), 1)
    sub = lax.broadcasted_iota(jnp.int32, (G, B), 0)
    out = []
    for g in range(n):
        base = g * G
        rows = groups[g]
        cols = [jnp.broadcast_to(rows[:, base + m:base + m + 1], (G, B)) for m in range(G)]
        a = {(k, m): splat(cols[m], k) for m in range(G) for k in range(m, G)}
        inv = {}
        low = {}
        for m in range(G):
            r = lax.rsqrt(a[m, m])
            inv[m, m] = r
            for k in range(m + 1, G):
                low[k, m] = a[k, m] * r
            for j in range(m + 1, G):
                for k in range(j, G):
                    a[k, j] = a[k, j] - low[k, m] * low[j, m]
            for j in range(m):
                total = low[m, j] * inv[j, j]
                for k in range(j + 1, m):
                    total = total + low[m, k] * inv[k, j]
                inv[m, j] = -total * r
        inside = (lane >= base) & (lane < base + G)
        unit = jnp.where(lane - base == sub, 1.0, 0.0).astype(jnp.float32)
        rows = jnp.where(inside, unit, rows)
        spread = [splat(rows, m) for m in range(G)]
        done = None
        for m in range(G):
            column = inv[m, m]
            for k in range(m + 1, G):
                column = jnp.where(sub == k, inv[k, m], column)
            column = jnp.where(sub < m, 0.0, column)
            term = column * spread[m]
            done = term if done is None else done + term
        out.append(jnp.where(lane < base + G, done, 0.0))
        if g + 1 == n:
            break
        spread_done = [splat(done, m) for m in range(G)]
        solved = []
        for j in range(G):
            total = None
            for m in range(j, G):
                term = inv[m, j] * spread_done[m]
                total = term if total is None else total + term
            solved.append(total)
        for h in range(g + 1, n):
            old = groups[h]
            new = jnp.where(inside, 0.0, old)
            for m in range(G):
                c = jnp.broadcast_to(old[:, base + m:base + m + 1], (G, B))
                new = new - c * solved[m]
            groups[h] = new
    return out


def dot(left, right):
    return jnp.dot(left, right, precision=HI, preferred_element_type=jnp.float32)


def factor_step_kernel(b, a_ref, o_ref, d_ref):
    start, end = b * B, (b + 1) * B
    block = a_ref[start:end, start:end]
    for g, rows in enumerate(factor_block([block[g * G:(g + 1) * G, :] for g in range(B // G)])):
        d_ref[g * G:(g + 1) * G, :] = rows
    inverse = d_ref[...]
    if b > 0:
        o_ref[:start, :] = a_ref[:start, :]
        before = dot(inverse, a_ref[start:end, :start])
        o_ref[start:end, :start] = before
    o_ref[start:end, start:end] = inverse
    if end < W:
        o_ref[start:end, end:] = jnp.zeros((B, W - end), jnp.float32)
        behind = dot(inverse, a_ref[start:end, end:])
        coef = lax.dot_general(
            a_ref[end:, start:end], inverse, (((1,), (1,)), ((), ())), precision=HI, preferred_element_type=jnp.float32
        )
        if b > 0:
            o_ref[end:, :start] = a_ref[end:, :start] - dot(coef, before)
        o_ref[end:, start:end] = -dot(coef, inverse)
        o_ref[end:, end:] = a_ref[end:, end:] - dot(coef, behind)


def factor_step(b, a):
    return pl.pallas_call(
        functools.partial(factor_step_kernel, b),
        out_shape=jax.ShapeDtypeStruct((W, W), jnp.float32),
        in_specs=[pl.BlockSpec(memory_space=pltpu.VMEM)],
        out_specs=pl.BlockSpec(memory_space=pltpu.VMEM),
        scratch_shapes=[pltpu.VMEM((B, B), jnp.float32)],
        name="factor_step",
    )(a)


BF, F32 = jnp.bfloat16, jnp.float32


def halves(value):
    high = value.astype(BF)
    return high, (value - high.astype(F32)).astype(BF)


def product(left_high, left_low, right_high, right_low):
    return (
        jnp.dot(left_high, right_high, preferred_element_type=F32)
        + jnp.dot(left_high, right_low, preferred_element_type=F32)
        + jnp.dot(left_low, right_high, preferred_element_type=F32)
    )


def split_factor(inverse_ref, high_ref, low_ref):
    high, low = halves(inverse_ref[...])
    high_ref[...] = high
    low_ref[...] = low


def own_kernel(inverse_ref, panel_ref, partner_ref, left_ref, slice_ref, lh, ll, ph, pq, xh, xl, xt):
    split_factor(inverse_ref, lh, ll)
    size = slice_ref.shape[0]
    col = lax.axis_index("col")
    for j, flip in enumerate(gathered_order(W // size)):
        to = pl.ds(pl.multiple_of(jnp.bitwise_xor(col, flip) * size, size), size)
        at = j * size % (W // 2)
        source = panel_ref if j * size < W // 2 else partner_ref
        high, low = halves(source[at:at + size, :])
        ph[to, :] = high
        pq[to, :] = low
    rows = panel_ref.shape[1]
    for top in range(0, W, 2 * B):
        depth = top + 2 * B
        for first in range(0, rows, 2 * B):
            cut = slice(first, first + 2 * B)
            xt[top:depth, cut] = product(
                lh[top:depth, :depth], ll[top:depth, :depth], ph[:depth, cut], pq[:depth, cut]
            )
    slice_ref[...] = xt[pl.ds(pl.multiple_of(col * size, size), size), :]
    for first in range(0, rows, B):
        for part in range(0, W, B):
            high, low = halves(xt[part:part + B, first:first + B].T)
            xh[first:first + B, part:part + B] = high
            xl[first:first + B, part:part + B] = low
    for first in range(0, rows, 2 * B):
        cut = slice(first, first + 2 * B)
        for top in range(0, W, 2 * B):
            across = slice(top, top + 2 * B)
            high, low = halves(product(xh[cut, top:], xl[cut, top:], lh[top:, across], ll[top:, across]))
            for part in range(2):
                left_ref[first // B + part, :B, across] = high[part * B:(part + 1) * B]
                left_ref[first // B + part, B:, across] = low[part * B:(part + 1) * B]


def tiles_kernel(reach, targets_ref, left_hbm, tiles_hbm, *refs):
    pieces, (out_hbm, left, far, tiles, out, right, in_sem, far_sem, out_sem) = refs[:len(reach)], refs[len(reach):]
    blocks, size = left.shape[0], far.shape[1]
    count = out.shape[0]
    col, row = lax.axis_index("col"), lax.axis_index("row")
    n_cols = lax.axis_size("col")
    side = lax.div(row, n_cols)
    starts = [0]
    for piece in pieces:
        starts.append(starts[-1] + piece.shape[0])
    far_copies = [
        pltpu.make_async_copy(piece, far.at[pl.ds(starts[i], piece.shape[0])], far_sem.at[i])
        for i, piece in enumerate(pieces)
    ]
    left_copy = pltpu.make_async_copy(left_hbm, left, in_sem.at[0])
    tiles_copy = pltpu.make_async_copy(tiles_hbm, tiles, in_sem.at[1])
    for copy in far_copies:
        copy.start()
    left_copy.start()
    tiles_copy.start()
    for i, (away, parts) in enumerate(reach):
        far_copies[i].wait()
        for place, part in enumerate(parts):
            copied, slot = part % COPIES, part // COPIES
            apart = lax.rem(row + away - col - copied * (n_cols // COPIES) + 4 * n_cols, n_cols)
            k = jnp.where(apart < n_cols // 2, 2 * apart, 2 * n_cols - 1 - 2 * apart)
            to = pl.ds(pl.multiple_of(k * size, size), size)
            high, low = halves(far[starts[i] + place])
            for block in range(blocks):
                right[slot * blocks + block, to, :B] = high[:, block * B:(block + 1) * B]
                right[slot * blocks + block, to, B:] = low[:, block * B:(block + 1) * B]
    left_copy.wait()
    tiles_copy.wait()

    def one(slot, carry):
        p = targets_ref[0, slot]
        q = targets_ref[1, slot]
        group = lax.rem(lax.div(lax.div(q, blocks), n_cols), 2)
        which = jnp.where(group == side, 0, 1) * blocks + lax.rem(q, blocks)
        four = jnp.dot(left[lax.rem(p, blocks)], right[which], preferred_element_type=F32)
        update = four[:B, :B] + (four[:B, B:] + four[B:, :B])
        tile = tiles[slot]
        out[slot] = jnp.where(p >= q, tile - update, tile)
        pltpu.make_async_copy(out.at[slot], out_hbm.at[slot], out_sem.at[slot]).start()
        return carry

    lax.fori_loop(0, count, one, 0, unroll=UNROLL)

    def drain(slot, carry):
        pltpu.make_async_copy(out.at[slot], out_hbm.at[slot], out_sem.at[slot]).wait()
        return carry

    lax.fori_loop(0, count, drain, 0)


def vmem(count):
    return [pl.BlockSpec(memory_space=pltpu.VMEM)] * count


def gathered_order(n_cols):
    order = [0]
    for flip in (n_cols // 4, n_cols // 8, n_cols // 2, 1):
        order += [entry ^ flip for entry in order]
    return order


def on_device(diag_block, panel, tiles, targets):
    n_rows, n_cols = lax.axis_size("row"), lax.axis_size("col")
    size, rows = panel.shape[1], panel.shape[0]
    blocks, count = rows // B, tiles.shape[0]
    mine = panel.T
    together = lax.optimization_barrier

    def at(r, c):
        return r * n_cols + c

    def moved(r, step):
        return r // n_cols * n_cols + (r + step) % n_cols

    def spread(c):
        return c // 2 if c % 2 == 0 else n_cols - 1 - c // 2

    everyone = [(r, c) for r in range(n_rows) for c in range(n_cols)]
    lift = [(at(r, c), at(r + n_cols, c)) for r, c in everyone if r < n_cols]
    up = [(r, moved(r, 1)) for r in range(n_rows)]
    down = [(r, moved(r, -1)) for r in range(n_rows)]
    flips = [[(c, c ^ flip) for c in range(n_cols)] for flip in (n_cols // 4, n_cols // 8, n_cols // 2, 1)]

    near = []
    for copied in range(COPIES):
        apart = copied * (n_cols // COPIES)
        pairs = [(at(r, c), at(moved(r, spread(c) + apart), r % n_cols)) for r, c in everyone]
        near.append(lax.ppermute(mine, ("row", "col"), pairs))
    own = mine
    received = lax.ppermute(own, "col", flips[0])
    work = factor_step(0, diag_block)
    received, work = together((received, work))
    own = jnp.concatenate([own, received])
    received = lax.ppermute(own, "col", flips[1])
    work = factor_step(1, work)
    near, work = together((near, work))

    near = jnp.stack(near)
    other = lax.ppermute(near, ("row", "col"), lift)
    work = factor_step(2, work)
    near, other, work, received = together((near, other, work, received))

    base = jnp.concatenate([near, other])
    own = jnp.concatenate([own, received])
    upward = lax.ppermute(base, "row", up)
    downward = lax.ppermute(base, "row", down)
    received = lax.ppermute(own, "col", flips[2])
    work = factor_step(3, work)
    received, work = together((received, work))
    own = jnp.concatenate([own, received])
    received = lax.ppermute(own, "col", flips[3])
    left, panel_slice = own_rows(work, own, received, size, blocks)
    upward, downward, left, panel_slice = together((upward, downward, left, panel_slice))

    last_up = lax.ppermute(upward[:COPIES], "row", up)
    last_down = lax.ppermute(downward[COPIES:], "row", down)
    whole = tuple(range(2 * COPIES))
    pieces = [base, upward, downward, last_up, last_down]
    reach = ((0, whole), (-1, whole), (1, whole), (-2, whole[:COPIES]), (2, whole[COPIES:]))
    any_space = pl.BlockSpec(memory_space=pl.ANY)
    schur = pl.pallas_call(
        functools.partial(tiles_kernel, reach),
        out_shape=jax.ShapeDtypeStruct(tiles.shape, F32),
        in_specs=[pl.BlockSpec(memory_space=pltpu.SMEM), *[any_space] * (2 + len(pieces))],
        out_specs=any_space,
        scratch_shapes=[
            pltpu.VMEM(left.shape, BF),
            pltpu.VMEM((sum(piece.shape[0] for piece in pieces), size, rows), F32),
            pltpu.VMEM(tiles.shape, F32),
            pltpu.VMEM(tiles.shape, F32),
            pltpu.VMEM((2 * blocks, W, 2 * B), BF),
            pltpu.SemaphoreType.DMA((2,)),
            pltpu.SemaphoreType.DMA((len(pieces),)),
            pltpu.SemaphoreType.DMA((count,)),
        ],
        name="schur_tiles",
    )(targets.T, left, tiles, *pieces)
    return panel_slice.T, schur


def own_rows(inverse, own, received, size, blocks):
    rows = own.shape[1]
    return pl.pallas_call(
        own_kernel,
        out_shape=(
            jax.ShapeDtypeStruct((blocks, 2 * B, W), BF),
            jax.ShapeDtypeStruct((size, rows), F32),
        ),
        in_specs=vmem(3),
        out_specs=tuple(vmem(2)),
        scratch_shapes=[
            *[pltpu.VMEM((W, W), BF)] * 2,
            *[pltpu.VMEM((W, rows), BF)] * 2,
            *[pltpu.VMEM((rows, W), BF)] * 2,
            pltpu.VMEM((W, rows), F32),
        ],
        name="own_rows",
    )(inverse, own, received)


def solution(mesh):
    placed = (P(), P("row", "col"), P(("row", "col"), None, None), P(("row", "col"), None))
    return jax.shard_map(
        on_device,
        mesh=mesh,
        in_specs=placed,
        out_specs=(P("row", "col"), P(("row", "col"), None, None)),
        check_vma=False,
    )
```

```python
import functools

import jax
import jax.numpy as jnp
from jax import lax
from jax.experimental import pallas as pl
from jax.experimental.pallas import tpu as pltpu
from jax.sharding import PartitionSpec as P

W, B, G, UNROLL, COPIES = 512, 128, 8, 4, 2
HI = lax.Precision.HIGHEST


def splat(col, k):
    return jnp.broadcast_to(col[k:k + 1, :], (G, B))


def factor_block(groups):
    n = len(groups)
    lane = lax.broadcasted_iota(jnp.int32, (G, B), 1)
    sub = lax.broadcasted_iota(jnp.int32, (G, B), 0)
    out = []
    for g in range(n):
        base = g * G
        rows = groups[g]
        cols = [jnp.broadcast_to(rows[:, base + m:base + m + 1], (G, B)) for m in range(G)]
        a = {(k, m): splat(cols[m], k) for m in range(G) for k in range(m, G)}
        inv = {}
        low = {}
        for m in range(G):
            r = lax.rsqrt(a[m, m])
            inv[m, m] = r
            for k in range(m + 1, G):
                low[k, m] = a[k, m] * r
            for j in range(m + 1, G):
                for k in range(j, G):
                    a[k, j] = a[k, j] - low[k, m] * low[j, m]
            for j in range(m):
                total = low[m, j] * inv[j, j]
                for k in range(j + 1, m):
                    total = total + low[m, k] * inv[k, j]
                inv[m, j] = -total * r
        inside = (lane >= base) & (lane < base + G)
        unit = jnp.where(lane - base == sub, 1.0, 0.0).astype(jnp.float32)
        rows = jnp.where(inside, unit, rows)
        spread = [splat(rows, m) for m in range(G)]
        done = None
        for m in range(G):
            column = inv[m, m]
            for k in range(m + 1, G):
                column = jnp.where(sub == k, inv[k, m], column)
            column = jnp.where(sub < m, 0.0, column)
            term = column * spread[m]
            done = term if done is None else done + term
        out.append(jnp.where(lane < base + G, done, 0.0))
        if g + 1 == n:
            break
        spread_done = [splat(done, m) for m in range(G)]
        solved = []
        for j in range(G):
            total = None
            for m in range(j, G):
                term = inv[m, j] * spread_done[m]
                total = term if total is None else total + term
            solved.append(total)
        for h in range(g + 1, n):
            old = groups[h]
            new = jnp.where(inside, 0.0, old)
            for m in range(G):
                c = jnp.broadcast_to(old[:, base + m:base + m + 1], (G, B))
                new = new - c * solved[m]
            groups[h] = new
    return out


def dot(left, right):
    return jnp.dot(left, right, precision=HI, preferred_element_type=jnp.float32)


def factor_step_kernel(b, a_ref, o_ref, d_ref):
    start, end = b * B, (b + 1) * B
    block = a_ref[start:end, start:end]
    for g, rows in enumerate(factor_block([block[g * G:(g + 1) * G, :] for g in range(B // G)])):
        d_ref[g * G:(g + 1) * G, :] = rows
    inverse = d_ref[...]
    if b > 0:
        o_ref[:start, :] = a_ref[:start, :]
        before = dot(inverse, a_ref[start:end, :start])
        o_ref[start:end, :start] = before
    o_ref[start:end, start:end] = inverse
    if end < W:
        o_ref[start:end, end:] = jnp.zeros((B, W - end), jnp.float32)
        behind = dot(inverse, a_ref[start:end, end:])
        coef = lax.dot_general(
            a_ref[end:, start:end], inverse, (((1,), (1,)), ((), ())), precision=HI, preferred_element_type=jnp.float32
        )
        if b > 0:
            o_ref[end:, :start] = a_ref[end:, :start] - dot(coef, before)
        o_ref[end:, start:end] = -dot(coef, inverse)
        o_ref[end:, end:] = a_ref[end:, end:] - dot(coef, behind)


def factor_step(b, a):
    return pl.pallas_call(
        functools.partial(factor_step_kernel, b),
        out_shape=jax.ShapeDtypeStruct((W, W), jnp.float32),
        in_specs=[pl.BlockSpec(memory_space=pltpu.VMEM)],
        out_specs=pl.BlockSpec(memory_space=pltpu.VMEM),
        scratch_shapes=[pltpu.VMEM((B, B), jnp.float32)],
        name="factor_step",
    )(a)


BF, F32 = jnp.bfloat16, jnp.float32


def halves(value):
    high = value.astype(BF)
    return high, (value - high.astype(F32)).astype(BF)


def product(left_high, left_low, right_high, right_low):
    return (
        jnp.dot(left_high, right_high, preferred_element_type=F32)
        + jnp.dot(left_high, right_low, preferred_element_type=F32)
        + jnp.dot(left_low, right_high, preferred_element_type=F32)
    )


def split_factor(inverse_ref, high_ref, low_ref):
    high, low = halves(inverse_ref[...])
    high_ref[...] = high
    low_ref[...] = low


def own_kernel(inverse_ref, panel_ref, partner_ref, left_ref, slice_ref, lh, ll, ph, pq, xh, xl, xt):
    split_factor(inverse_ref, lh, ll)
    size = slice_ref.shape[0]
    col = lax.axis_index("col")
    for j, flip in enumerate(gathered_order(W // size)):
        to = pl.ds(pl.multiple_of(jnp.bitwise_xor(col, flip) * size, size), size)
        at = j * size % (W // 2)
        source = panel_ref if j * size < W // 2 else partner_ref
        high, low = halves(source[at:at + size, :])
        ph[to, :] = high
        pq[to, :] = low
    rows = panel_ref.shape[1]
    for top in range(0, W, 2 * B):
        depth = top + 2 * B
        for first in range(0, rows, 2 * B):
            cut = slice(first, first + 2 * B)
            xt[top:depth, cut] = product(
                lh[top:depth, :depth], ll[top:depth, :depth], ph[:depth, cut], pq[:depth, cut]
            )
    slice_ref[...] = xt[pl.ds(pl.multiple_of(col * size, size), size), :]
    for first in range(0, rows, B):
        for part in range(0, W, B):
            high, low = halves(xt[part:part + B, first:first + B].T)
            xh[first:first + B, part:part + B] = high
            xl[first:first + B, part:part + B] = low
    for first in range(0, rows, 2 * B):
        cut = slice(first, first + 2 * B)
        for top in range(0, W, 2 * B):
            across = slice(top, top + 2 * B)
            high, low = halves(product(xh[cut, top:], xl[cut, top:], lh[top:, across], ll[top:, across]))
            for part in range(2):
                left_ref[first // B + part, :B, across] = high[part * B:(part + 1) * B]
                left_ref[first // B + part, B:, across] = low[part * B:(part + 1) * B]


def tiles_kernel(reach, targets_ref, left_hbm, tiles_hbm, *refs):
    pieces, (out_hbm, left, far, tiles, out, right, in_sem, far_sem, out_sem) = refs[:len(reach)], refs[len(reach):]
    blocks, size = left.shape[0], far.shape[1]
    count = out.shape[0]
    col, row = lax.axis_index("col"), lax.axis_index("row")
    n_cols = lax.axis_size("col")
    side = lax.div(row, n_cols)
    starts = [0]
    for piece in pieces:
        starts.append(starts[-1] + piece.shape[0])
    far_copies = [
        pltpu.make_async_copy(piece, far.at[pl.ds(starts[i], piece.shape[0])], far_sem.at[i])
        for i, piece in enumerate(pieces)
    ]
    left_copy = pltpu.make_async_copy(left_hbm, left, in_sem.at[0])
    tiles_copy = pltpu.make_async_copy(tiles_hbm, tiles, in_sem.at[1])
    for copy in far_copies:
        copy.start()
    left_copy.start()
    tiles_copy.start()
    for i, (away, parts) in enumerate(reach):
        far_copies[i].wait()
        for place, part in enumerate(parts):
            copied, slot = part % COPIES, part // COPIES
            apart = lax.rem(row + away - col - copied * (n_cols // COPIES) + 4 * n_cols, n_cols)
            k = jnp.where(apart < n_cols // 2, 2 * apart, 2 * n_cols - 1 - 2 * apart)
            to = pl.ds(pl.multiple_of(k * size, size), size)
            high, low = halves(far[starts[i] + place])
            for block in range(blocks):
                right[slot * blocks + block, to, :B] = high[:, block * B:(block + 1) * B]
                right[slot * blocks + block, to, B:] = low[:, block * B:(block + 1) * B]
    left_copy.wait()
    tiles_copy.wait()

    def one(slot, carry):
        p = targets_ref[0, slot]
        q = targets_ref[1, slot]
        group = lax.rem(lax.div(lax.div(q, blocks), n_cols), 2)
        which = jnp.where(group == side, 0, 1) * blocks + lax.rem(q, blocks)
        four = jnp.dot(left[lax.rem(p, blocks)], right[which], preferred_element_type=F32)
        update = four[:B, :B] + (four[:B, B:] + four[B:, :B])
        tile = tiles[slot]
        out[slot] = jnp.where(p >= q, tile - update, tile)
        pltpu.make_async_copy(out.at[slot], out_hbm.at[slot], out_sem.at[slot]).start()
        return carry

    lax.fori_loop(0, count, one, 0, unroll=UNROLL)

    def drain(slot, carry):
        pltpu.make_async_copy(out.at[slot], out_hbm.at[slot], out_sem.at[slot]).wait()
        return carry

    lax.fori_loop(0, count, drain, 0)


def vmem(count):
    return [pl.BlockSpec(memory_space=pltpu.VMEM)] * count


def gathered_order(n_cols):
    order = [0]
    for flip in (n_cols // 4, n_cols // 8, n_cols // 2, 1):
        order += [entry ^ flip for entry in order]
    return order


def on_device(diag_block, panel, tiles, targets):
    n_rows, n_cols = lax.axis_size("row"), lax.axis_size("col")
    size, rows = panel.shape[1], panel.shape[0]
    blocks, count = rows // B, tiles.shape[0]
    mine = panel.T
    half = n_cols // 2
    together = lax.optimization_barrier

    def at(r, c):
        return r * n_cols + c

    def moved(r, step):
        return r // n_cols * n_cols + (r + step) % n_cols

    def spread(c):
        return c // 2 if c % 2 == 0 else n_cols - 1 - c // 2

    everyone = [(r, c) for r in range(n_rows) for c in range(n_cols)]
    turn = [(at(r, c), at(moved(r, spread(c)), r % n_cols)) for r, c in everyone]
    twin = [(at(r, c), at(moved(r, spread(c) + half), r % n_cols)) for r, c in everyone]
    lift = [(at(r, c), at(r + n_cols, c)) for r, c in everyone if r < n_cols]
    up = [(r, moved(r, 1)) for r in range(n_rows)]
    down = [(r, moved(r, -1)) for r in range(n_rows)]
    flips = [[(c, c ^ flip) for c in range(n_cols)] for flip in (n_cols // 4, n_cols // 8, n_cols // 2, 1)]

    received = lax.ppermute(mine, "col", flips[0])
    first = lax.ppermute(mine, ("row", "col"), turn)
    second = lax.ppermute(mine, ("row", "col"), twin)
    work = factor_step(0, diag_block)
    first, second, work, received = together((first, second, work, received))

    near = jnp.stack([first, second])
    other = lax.ppermute(near, ("row", "col"), lift)
    own = jnp.concatenate([mine, received])
    received = lax.ppermute(own, "col", flips[1])
    near, other, work = together((near, other, work))

    base = jnp.concatenate([near, other])
    whole = tuple(range(2 * COPIES))
    upward, downward, pieces, reach = base, base, [base], [(0, whole)]
    for step in range(1, half // 2 + 1):
        both = step < half // 2
        if not both:
            upward, downward = upward[:COPIES], downward[COPIES:]
        upward = lax.ppermute(upward, "row", up)
        downward = lax.ppermute(downward, "row", down)
        if step < W // B:
            work = factor_step(step, work)
            received, work = together((received, work))
            if step + 1 < W // B:
                own = jnp.concatenate([own, received])
                received = lax.ppermute(own, "col", flips[step + 1])
            else:
                left, panel_slice = own_rows(work, own, received, size, blocks)
            upward, downward, work = together((upward, downward, work))
        else:
            upward, downward, left, panel_slice = together((upward, downward, left, panel_slice))
        pieces += [upward, downward]
        reach += [(-step, whole if both else whole[:COPIES]), (step, whole if both else whole[COPIES:])]
    any_space = pl.BlockSpec(memory_space=pl.ANY)
    schur = pl.pallas_call(
        functools.partial(tiles_kernel, tuple(reach)),
        out_shape=jax.ShapeDtypeStruct(tiles.shape, F32),
        in_specs=[pl.BlockSpec(memory_space=pltpu.SMEM), *[any_space] * (2 + len(pieces))],
        out_specs=any_space,
        scratch_shapes=[
            pltpu.VMEM(left.shape, BF),
            pltpu.VMEM((sum(piece.shape[0] for piece in pieces), size, rows), F32),
            pltpu.VMEM(tiles.shape, F32),
            pltpu.VMEM(tiles.shape, F32),
            pltpu.VMEM((2 * blocks, W, 2 * B), BF),
            pltpu.SemaphoreType.DMA((2,)),
            pltpu.SemaphoreType.DMA((len(pieces),)),
            pltpu.SemaphoreType.DMA((count,)),
        ],
        name="schur_tiles",
    )(targets.T, left, tiles, *pieces)
    return panel_slice.T, schur


def own_rows(inverse, own, received, size, blocks):
    rows = own.shape[1]
    return pl.pallas_call(
        own_kernel,
        out_shape=(
            jax.ShapeDtypeStruct((blocks, 2 * B, W), BF),
            jax.ShapeDtypeStruct((size, rows), F32),
        ),
        in_specs=vmem(3),
        out_specs=tuple(vmem(2)),
        scratch_shapes=[
            *[pltpu.VMEM((W, W), BF)] * 2,
            *[pltpu.VMEM((W, rows), BF)] * 2,
            *[pltpu.VMEM((rows, W), BF)] * 2,
            pltpu.VMEM((W, rows), F32),
        ],
        name="own_rows",
    )(inverse, own, received)


def solution(mesh):
    placed = (P(), P("row", "col"), P(("row", "col"), None, None), P(("row", "col"), None))
    return jax.shard_map(
        on_device,
        mesh=mesh,
        in_specs=placed,
        out_specs=(P("row", "col"), P(("row", "col"), None, None)),
        check_vma=False,
    )
```

```python
import functools

import jax
import jax.numpy as jnp
from jax import lax
from jax.experimental import pallas as pl
from jax.experimental.pallas import tpu as pltpu
from jax.sharding import PartitionSpec as P

W, B, G, UNROLL, COPIES = 512, 128, 8, 4, 2
HI = lax.Precision.HIGHEST


def splat(col, k):
    return jnp.broadcast_to(col[k:k + 1, :], (G, B))


def factor_block(groups):
    n = len(groups)
    lane = lax.broadcasted_iota(jnp.int32, (G, B), 1)
    sub = lax.broadcasted_iota(jnp.int32, (G, B), 0)
    out = []
    for g in range(n):
        base = g * G
        rows = groups[g]
        cols = [jnp.broadcast_to(rows[:, base + m:base + m + 1], (G, B)) for m in range(G)]
        a = {(k, m): splat(cols[m], k) for m in range(G) for k in range(m, G)}
        inv = {}
        low = {}
        for m in range(G):
            r = lax.rsqrt(a[m, m])
            inv[m, m] = r
            for k in range(m + 1, G):
                low[k, m] = a[k, m] * r
            for j in range(m + 1, G):
                for k in range(j, G):
                    a[k, j] = a[k, j] - low[k, m] * low[j, m]
            for j in range(m):
                total = low[m, j] * inv[j, j]
                for k in range(j + 1, m):
                    total = total + low[m, k] * inv[k, j]
                inv[m, j] = -total * r
        inside = (lane >= base) & (lane < base + G)
        unit = jnp.where(lane - base == sub, 1.0, 0.0).astype(jnp.float32)
        rows = jnp.where(inside, unit, rows)
        spread = [splat(rows, m) for m in range(G)]
        done = None
        for m in range(G):
            column = inv[m, m]
            for k in range(m + 1, G):
                column = jnp.where(sub == k, inv[k, m], column)
            column = jnp.where(sub < m, 0.0, column)
            term = column * spread[m]
            done = term if done is None else done + term
        out.append(jnp.where(lane < base + G, done, 0.0))
        if g + 1 == n:
            break
        spread_done = [splat(done, m) for m in range(G)]
        solved = []
        for j in range(G):
            total = None
            for m in range(j, G):
                term = inv[m, j] * spread_done[m]
                total = term if total is None else total + term
            solved.append(total)
        for h in range(g + 1, n):
            old = groups[h]
            new = jnp.where(inside, 0.0, old)
            for m in range(G):
                c = jnp.broadcast_to(old[:, base + m:base + m + 1], (G, B))
                new = new - c * solved[m]
            groups[h] = new
    return out


def dot(left, right):
    return jnp.dot(left, right, precision=HI, preferred_element_type=jnp.float32)


def factor_step_kernel(b, a_ref, o_ref, d_ref):
    start, end = b * B, (b + 1) * B
    block = a_ref[start:end, start:end]
    for g, rows in enumerate(factor_block([block[g * G:(g + 1) * G, :] for g in range(B // G)])):
        d_ref[g * G:(g + 1) * G, :] = rows
    inverse = d_ref[...]
    if b > 0:
        o_ref[:start, :] = a_ref[:start, :]
        before = dot(inverse, a_ref[start:end, :start])
        o_ref[start:end, :start] = before
    o_ref[start:end, start:end] = inverse
    if end < W:
        o_ref[start:end, end:] = jnp.zeros((B, W - end), jnp.float32)
        behind = dot(inverse, a_ref[start:end, end:])
        coef = lax.dot_general(
            a_ref[end:, start:end], inverse, (((1,), (1,)), ((), ())), precision=HI, preferred_element_type=jnp.float32
        )
        if b > 0:
            o_ref[end:, :start] = a_ref[end:, :start] - dot(coef, before)
        o_ref[end:, start:end] = -dot(coef, inverse)
        o_ref[end:, end:] = a_ref[end:, end:] - dot(coef, behind)


def factor_step(b, a):
    return pl.pallas_call(
        functools.partial(factor_step_kernel, b),
        out_shape=pltpu.VMEM((W, W), jnp.float32),
        in_specs=[pl.BlockSpec(memory_space=pltpu.VMEM)],
        out_specs=pl.BlockSpec(memory_space=pltpu.VMEM),
        scratch_shapes=[pltpu.VMEM((B, B), jnp.float32)],
        compiler_params=pltpu.CompilerParams(vmem_limit_bytes=24 << 20),
        name="factor_step",
    )(pltpu.with_memory_space_constraint(a, pltpu.VMEM))


BF, F32 = jnp.bfloat16, jnp.float32


def halves(value):
    high = value.astype(BF)
    return high, (value - high.astype(F32)).astype(BF)


def product(left_high, left_low, right_high, right_low):
    return (
        jnp.dot(left_high, right_high, preferred_element_type=F32)
        + jnp.dot(left_high, right_low, preferred_element_type=F32)
        + jnp.dot(left_low, right_high, preferred_element_type=F32)
    )


def split_factor(inverse_ref, high_ref, low_ref):
    high, low = halves(inverse_ref[...])
    high_ref[...] = high
    low_ref[...] = low


def own_kernel(inverse_ref, panel_ref, partner_ref, left_ref, slice_ref, lh, ll, ph, pq, xh, xl, xt):
    split_factor(inverse_ref, lh, ll)
    size = slice_ref.shape[0]
    col = lax.axis_index("col")
    for j, flip in enumerate(gathered_order(W // size)):
        to = pl.ds(pl.multiple_of(jnp.bitwise_xor(col, flip) * size, size), size)
        at = j * size % (W // 2)
        source = panel_ref if j * size < W // 2 else partner_ref
        high, low = halves(source[at:at + size, :])
        ph[to, :] = high
        pq[to, :] = low
    rows = panel_ref.shape[1]
    for top in range(0, W, 2 * B):
        depth = top + 2 * B
        for first in range(0, rows, 2 * B):
            cut = slice(first, first + 2 * B)
            xt[top:depth, cut] = product(
                lh[top:depth, :depth], ll[top:depth, :depth], ph[:depth, cut], pq[:depth, cut]
            )
    slice_ref[...] = xt[pl.ds(pl.multiple_of(col * size, size), size), :]
    for first in range(0, rows, B):
        for part in range(0, W, B):
            high, low = halves(xt[part:part + B, first:first + B].T)
            xh[first:first + B, part:part + B] = high
            xl[first:first + B, part:part + B] = low
    for first in range(0, rows, 2 * B):
        cut = slice(first, first + 2 * B)
        for top in range(0, W, 2 * B):
            across = slice(top, top + 2 * B)
            high, low = halves(product(xh[cut, top:], xl[cut, top:], lh[top:, across], ll[top:, across]))
            for part in range(2):
                left_ref[first // B + part, :B, across] = high[part * B:(part + 1) * B]
                left_ref[first // B + part, B:, across] = low[part * B:(part + 1) * B]


def tiles_kernel(reach, targets_ref, tiles_hbm, left, *refs):
    pieces, (out_hbm, tiles, out, right, in_sem, out_sem) = refs[:len(reach)], refs[len(reach):]
    blocks, size = left.shape[0], pieces[0].shape[1]
    count = out.shape[0]
    col, row = lax.axis_index("col"), lax.axis_index("row")
    n_cols = lax.axis_size("col")
    side = lax.div(row, n_cols)
    tiles_copy = pltpu.make_async_copy(tiles_hbm, tiles, in_sem)
    tiles_copy.start()
    for i, (away, parts) in enumerate(reach):
        for place, part in enumerate(parts):
            copied, slot = part % COPIES, part // COPIES
            apart = lax.rem(row + away - col - copied * (n_cols // COPIES) + 4 * n_cols, n_cols)
            k = jnp.where(apart < n_cols // 2, 2 * apart, 2 * n_cols - 1 - 2 * apart)
            to = pl.ds(pl.multiple_of(k * size, size), size)
            high, low = halves(pieces[i][place])
            for block in range(blocks):
                right[slot * blocks + block, to, :B] = high[:, block * B:(block + 1) * B]
                right[slot * blocks + block, to, B:] = low[:, block * B:(block + 1) * B]
    tiles_copy.wait()

    def one(slot, carry):
        p = targets_ref[0, slot]
        q = targets_ref[1, slot]
        group = lax.rem(lax.div(lax.div(q, blocks), n_cols), 2)
        which = jnp.where(group == side, 0, 1) * blocks + lax.rem(q, blocks)
        four = jnp.dot(left[lax.rem(p, blocks)], right[which], preferred_element_type=F32)
        update = four[:B, :B] + (four[:B, B:] + four[B:, :B])
        tile = tiles[slot]
        out[slot] = jnp.where(p >= q, tile - update, tile)
        pltpu.make_async_copy(out.at[slot], out_hbm.at[slot], out_sem.at[slot]).start()
        return carry

    lax.fori_loop(0, count, one, 0, unroll=UNROLL)

    def drain(slot, carry):
        pltpu.make_async_copy(out.at[slot], out_hbm.at[slot], out_sem.at[slot]).wait()
        return carry

    lax.fori_loop(0, count, drain, 0)


def vmem(count):
    return [pl.BlockSpec(memory_space=pltpu.VMEM)] * count


def gathered_order(n_cols):
    order = [0]
    for flip in (n_cols // 4, n_cols // 8, n_cols // 2, 1):
        order += [entry ^ flip for entry in order]
    return order


def near_core(value):
    return pltpu.with_memory_space_constraint(value, pltpu.VMEM)


def on_device(diag_block, panel, tiles, targets):
    n_rows, n_cols = lax.axis_size("row"), lax.axis_size("col")
    size, rows = panel.shape[1], panel.shape[0]
    blocks, count = rows // B, tiles.shape[0]
    mine = panel.T
    half = n_cols // 2
    together = lax.optimization_barrier

    def at(r, c):
        return r * n_cols + c

    def moved(r, step):
        return r // n_cols * n_cols + (r + step) % n_cols

    def spread(c):
        return c // 2 if c % 2 == 0 else n_cols - 1 - c // 2

    everyone = [(r, c) for r in range(n_rows) for c in range(n_cols)]
    turn = [(at(r, c), at(moved(r, spread(c)), r % n_cols)) for r, c in everyone]
    twin = [(at(r, c), at(moved(r, spread(c) + half), r % n_cols)) for r, c in everyone]
    lift = [(at(r, c), at(r + n_cols, c)) for r, c in everyone if r < n_cols]
    up = [(r, moved(r, 1)) for r in range(n_rows)]
    down = [(r, moved(r, -1)) for r in range(n_rows)]
    flips = [[(c, c ^ flip) for c in range(n_cols)] for flip in (n_cols // 4, n_cols // 8, n_cols // 2, 1)]

    first = lax.ppermute(mine, ("row", "col"), turn)
    second = lax.ppermute(mine, ("row", "col"), twin)
    received = lax.ppermute(mine, "col", flips[0])
    work = factor_step(0, diag_block)
    first, second, work, received = together((first, second, work, received))

    near = jnp.stack([first, second])
    other = lax.ppermute(near, ("row", "col"), lift)
    own = jnp.concatenate([mine, received])
    received = lax.ppermute(own, "col", flips[1])
    near, other, work = together((near, other, work))

    base = jnp.concatenate([near, other])
    whole = tuple(range(2 * COPIES))
    upward, downward, pieces, reach = base, base, [base], [(0, whole)]
    for step in range(1, half // 2 + 1):
        both = step < half // 2
        if not both:
            upward, downward = upward[:COPIES], downward[COPIES:]
        upward = lax.ppermute(upward, "row", up)
        downward = lax.ppermute(downward, "row", down)
        if step < W // B:
            work = factor_step(step, work)
            received, work = together((received, work))
            if step + 1 < W // B:
                own = jnp.concatenate([own, received])
                received = lax.ppermute(own, "col", flips[step + 1])
            else:
                left, panel_slice = own_rows(work, own, received, size, blocks)
            upward, downward, work = together((upward, downward, work))
        else:
            upward, downward, left, panel_slice = together((upward, downward, left, panel_slice))
        pieces += [upward, downward]
        reach += [(-step, whole if both else whole[:COPIES]), (step, whole if both else whole[COPIES:])]
    any_space = pl.BlockSpec(memory_space=pl.ANY)
    schur = pl.pallas_call(
        functools.partial(tiles_kernel, tuple(reach)),
        out_shape=jax.ShapeDtypeStruct(tiles.shape, F32),
        in_specs=[pl.BlockSpec(memory_space=pltpu.SMEM), any_space, *vmem(1 + len(pieces))],
        out_specs=any_space,
        scratch_shapes=[
            pltpu.VMEM(tiles.shape, F32),
            pltpu.VMEM(tiles.shape, F32),
            pltpu.VMEM((2 * blocks, W, 2 * B), BF),
            pltpu.SemaphoreType.DMA,
            pltpu.SemaphoreType.DMA((count,)),
        ],
        compiler_params=pltpu.CompilerParams(vmem_limit_bytes=24 << 20),
        name="schur_tiles",
    )(targets.T, tiles, *[near_core(value) for value in (left, *pieces)])
    return panel_slice.T, schur


def own_rows(inverse, own, received, size, blocks):
    rows = own.shape[1]
    return pl.pallas_call(
        own_kernel,
        out_shape=(
            pltpu.VMEM((blocks, 2 * B, W), BF),
            jax.ShapeDtypeStruct((size, rows), F32),
        ),
        in_specs=vmem(3),
        out_specs=tuple(vmem(2)),
        scratch_shapes=[
            *[pltpu.VMEM((W, W), BF)] * 2,
            *[pltpu.VMEM((W, rows), BF)] * 2,
            *[pltpu.VMEM((rows, W), BF)] * 2,
            pltpu.VMEM((W, rows), F32),
        ],
        compiler_params=pltpu.CompilerParams(vmem_limit_bytes=24 << 20),
        name="own_rows",
    )(near_core(inverse), near_core(own), near_core(received))


def solution(mesh):
    placed = (P(), P("row", "col"), P(("row", "col"), None, None), P(("row", "col"), None))
    return jax.shard_map(
        on_device,
        mesh=mesh,
        in_specs=placed,
        out_specs=(P("row", "col"), P(("row", "col"), None, None)),
        check_vma=False,
    )
```
